32 devices in a mesh: groups: 2 (over x), fsdp: 16 (over z, y, core).
Axes of the slice: x: 2, y: 2, z: 4, core: 2. Of those that a mesh axis runs over, the one named last changes fastest.
Arguments:
- layer_input: bfloat16 [512, 8192], P('groups', 'fsdp'), parts along dimension 0, may hold values from -6 to 6
- norm_gain: bfloat16 [8192], P('fsdp'), may hold values from 0.099609375 to 1.8984375
- w_query: bfloat16 [8192, 8192], P(None, 'fsdp'), may hold values from -0.0625 to 0.0625
- w_key: bfloat16 [8192, 1024], P('fsdp'), may hold values from -0.09375 to 0.09375
- w_value: bfloat16 [8192, 1024], P('fsdp'), may hold values from -0.09375 to 0.09375
- w_out: bfloat16 [8192, 8192], P('fsdp'), may hold values from -0.0625 to 0.0625
- cart_key: bfloat16 [4096, 1024], P(('groups', 'fsdp')), parts along dimension 0, may hold values from -100 to 100
- cart_value: bfloat16 [4096, 1024], P(('groups', 'fsdp')), parts along dimension 0, may hold values from -6 to 6
- grad_out: bfloat16 [512, 8192], P('groups', 'fsdp'), parts along dimension 0, may hold values from -6 to 6
Outputs:
- attn_out: bfloat16 [512, 8192], P('groups', 'fsdp'), parts along dimension 0
- grad_key: float32 [4096, 1024], P(('groups', 'fsdp')), parts along dimension 0
- grad_value: float32 [4096, 1024], P(('groups', 'fsdp')), parts along dimension 0
- new_keys: bfloat16 [512, 1024], P('groups', 'fsdp'), parts along dimension 0
- new_values: bfloat16 [512, 1024], P('groups', 'fsdp'), parts along dimension 0
The draws below stay inside these ranges and needn't reach their ends.
There are 2 independent parts, one for each index of `groups`. The reference program is written for one: setup_inputs(seed, part) draws one part's arguments, and reference() takes and returns one part's arrays. A program takes and returns all parts, laid end to end along the dimension named above; an argument that names none is the same for every part. Nothing has to cross between parts.
All inputs are finite; a program needn't handle non-finite values.
Results may differ from the reference program's by a relative error of at most 0.015.
The reference program's roundings to bfloat16 on the way count: a program that leaves them out, or rounds other values in their place, can miss the bound.
Values may be sent and summed in bfloat16 or wider, within the bound.
A program may use at most 128 MiB of HBM per device.

```python
import jax
import jax.numpy as jnp
from jax import lax

D = 8192
H = 64
KV = 8
HD = 128
C = 2048
SEQ = 64
TOKENS = 256


def draw_cart_key(key, part):
    first_key = jax.random.fold_in(key, 0)
    drawn = jnp.clip(jax.random.normal(first_key, (C, KV * HD), jnp.float32), -6.0, 6.0)
    return drawn.astype(jnp.bfloat16)


def spiked(array, own_key, source, target, parts, factor):
    owner, partner = [(jnp.arange(array.shape[position]) // (array.shape[position] // parts)).reshape([-1 if axis == position else 1 for axis in range(array.ndim)]) for position in (source, target)]
    chosen = jax.random.permutation(own_key, parts)[partner]
    strong = (owner == chosen) | (owner == (partner + parts // 2) % parts)
    return jnp.where(strong, factor * array, array)


def levels(key, shape, cuts, low, largest):
    loudness, own = 1.0, jax.random.fold_in(key, 6)
    for position, shards_of in cuts:
        heights = jnp.exp(jax.random.uniform(jax.random.fold_in(own, position), (shards_of,), jnp.float32, low / len(cuts), largest / len(cuts)))
        loudness = loudness * jnp.repeat(heights, shape[position] // shards_of).reshape([-1 if axis == position else 1 for axis in range(len(shape))])
    return loudness


def gaussian(own_key, extent, spread, reach, cuts=(), held_as=jnp.bfloat16):
    array = spread * jax.random.normal(own_key, extent, jnp.float32)
    if cuts:
        array = array * levels(own_key, extent, cuts, -0.22, 0.18)
    return jnp.clip(array, -reach, reach).astype(held_as)


def noise_with(stream_key, dims, spread, limit, shards, heavy, held_as=jnp.bfloat16):
    drawn = spread * jax.random.normal(stream_key, dims, jnp.float32)
    if shards:
        drawn = drawn * levels(stream_key, dims, shards, -0.22, 0.18)
    return jnp.clip(spiked(drawn, jax.random.fold_in(stream_key, 3), *heavy), -limit, limit).astype(held_as)


def setup_inputs(seed: int = 0, part: int = 0) -> dict:
    key_list = jax.random.split(jax.random.key(seed), 10)
    part_keys = jax.random.split(jax.random.fold_in(key_list[9], part), 10)
    layer_input = gaussian(part_keys[0], (TOKENS, D), 1.0, 6.0, ((1, 16),))
    norm_gain = jnp.clip(1.0 + 0.18 * jax.random.normal(key_list[1], (D,), jnp.float32), 0.099609375, 1.8984375).astype(jnp.bfloat16)
    w_query = gaussian(key_list[2], (D, H * HD), D ** -0.5, 0.0625, ((1, 16),))
    w_key = noise_with(key_list[3], (D, KV * HD), D ** -0.5, 0.09375, ((0, 16),), (0, 1, 16, 2.0))
    w_value = noise_with(key_list[4], (D, KV * HD), D ** -0.5, 0.09375, ((0, 16),), (0, 1, 16, 2.0))
    w_out = gaussian(key_list[5], (H * HD, D), (H * HD) ** -0.5, 0.0625, ((0, 16),))
    cart_key = draw_cart_key(jax.random.fold_in(jax.random.fold_in(key_list[9], part), 71), part)
    cart_value = gaussian(part_keys[7], (C, KV * HD), 1.0, 6.0, ((0, 16),))
    grad_out = gaussian(part_keys[8], (TOKENS, D), 1.0, 6.0, ((1, 16),))
    return dict(layer_input=layer_input, norm_gain=norm_gain, w_query=w_query, w_key=w_key, w_value=w_value, w_out=w_out, cart_key=cart_key, cart_value=cart_value, grad_out=grad_out)


def rotate(vectors, positions):
    half_dim = vectors.shape[-1] // 2
    frequency = jnp.exp(-jnp.log(500000.0) * jnp.arange(half_dim, dtype=jnp.float32) * (2.0 / vectors.shape[-1]))
    angles = positions.astype(jnp.float32)[:, None] * frequency[None, :]
    cosines = jnp.cos(angles)[:, None, :]
    sine_table = jnp.sin(angles)[:, None, :]
    first_half = vectors[..., :half_dim]
    second = vectors[..., half_dim:]
    return jnp.concatenate([first_half * cosines - second * sine_table, second * cosines + first_half * sine_table], -1)

def head_block(queries, slot_keys, slot_values, token_keys, token_values, grad_heads, seq_len):
    scaling = queries.shape[-1] ** (-0.5)
    token_count = queries.shape[1]
    query_f32 = queries.astype(jnp.float32)
    score_cart = jnp.einsum('gtd,cd->gtc', query_f32, slot_keys.astype(jnp.float32)) * scaling
    score_tok = jnp.einsum('gtd,sd->gts', query_f32, token_keys.astype(jnp.float32)) * scaling
    index_rows = jnp.arange(token_count)
    causal = (index_rows[:, None] // seq_len == index_rows[None, :] // seq_len) & (index_rows[None, :] <= index_rows[:, None])
    score_tok = jnp.where(causal[None], score_tok, -jnp.inf)
    row_max = jnp.maximum(lax.optimization_barrier(jnp.max(score_cart, -1, keepdims=True)), lax.optimization_barrier(jnp.max(score_tok, -1, keepdims=True)))
    exp_cart = jnp.exp(score_cart - row_max)
    exp_tok = jnp.exp(score_tok - row_max)
    totals = lax.optimization_barrier(jnp.sum(exp_cart, -1, keepdims=True)) + lax.optimization_barrier(jnp.sum(exp_tok, -1, keepdims=True))
    prob_cart = exp_cart / totals
    prob_tok = exp_tok / totals
    rounded_cart = prob_cart.astype(jnp.bfloat16)
    rounded_tok = prob_tok.astype(jnp.bfloat16)
    mixture = jnp.einsum('gtc,cd->gtd', rounded_cart.astype(jnp.float32), slot_values.astype(jnp.float32))
    mixture = mixture + jnp.einsum('gts,sd->gtd', rounded_tok.astype(jnp.float32), token_values.astype(jnp.float32))
    outputs = mixture.astype(jnp.bfloat16)
    grad_f32 = grad_heads.astype(jnp.float32)
    grad_prob_cart = jnp.einsum('gtd,cd->gtc', grad_f32, slot_values.astype(jnp.float32))
    deltas = lax.optimization_barrier(jnp.sum(grad_f32 * outputs.astype(jnp.float32), -1, keepdims=True))
    grad_score = (prob_cart * (grad_prob_cart - deltas)).astype(jnp.bfloat16)
    grad_keys = jnp.einsum('gtc,gtd->cd', grad_score.astype(jnp.float32), query_f32) * scaling
    grad_values = jnp.einsum('gtc,gtd->cd', rounded_cart.astype(jnp.float32), grad_f32)
    return (outputs, grad_keys, grad_values)

def reference(layer_input, norm_gain, w_query, w_key, w_value, w_out, cart_key, cart_value, grad_out):
    token_count = layer_input.shape[0]
    group_size = H // KV
    input_f32 = layer_input.astype(jnp.float32)
    inverse_rms = lax.rsqrt(lax.optimization_barrier(jnp.mean(input_f32 * input_f32, -1, keepdims=True)) + 1e-05)
    normed = (input_f32 * inverse_rms * norm_gain.astype(jnp.float32)[None, :]).astype(jnp.bfloat16)
    positions = C + jnp.arange(token_count) % SEQ
    queries = jnp.dot(normed, w_query, preferred_element_type=jnp.float32).reshape(token_count, H, HD)
    queries = rotate(queries, positions).astype(jnp.bfloat16)
    token_keys = jnp.dot(normed, w_key, preferred_element_type=jnp.float32).reshape(token_count, KV, HD)
    token_keys = rotate(token_keys, positions).astype(jnp.bfloat16)
    token_values = jnp.dot(normed, w_value, preferred_element_type=jnp.float32).astype(jnp.bfloat16).reshape(token_count, KV, HD)
    grad_heads = jnp.dot(grad_out, w_out.T, preferred_element_type=jnp.float32).astype(jnp.bfloat16)
    query_groups = queries.reshape(token_count, KV, group_size, HD).transpose(1, 2, 0, 3)
    grad_groups = grad_heads.reshape(token_count, KV, group_size, HD).transpose(1, 2, 0, 3)
    slot_keys = cart_key.reshape(C, KV, HD).transpose(1, 0, 2)
    slot_values = cart_value.reshape(C, KV, HD).transpose(1, 0, 2)

    def one_group(pieces):
        return head_block(pieces[0], pieces[1], pieces[2], pieces[3], pieces[4], pieces[5], SEQ)
    outputs, grad_keys, grad_values = lax.map(one_group, (query_groups, slot_keys, slot_values, token_keys.transpose(1, 0, 2), token_values.transpose(1, 0, 2), grad_groups))
    head_outputs = outputs.transpose(2, 0, 1, 3).reshape(token_count, H * HD)
    attn_out = jnp.dot(head_outputs, w_out, preferred_element_type=jnp.float32).astype(jnp.bfloat16)
    grad_key = grad_keys.transpose(1, 0, 2).reshape(C, KV * HD)
    grad_value = grad_values.transpose(1, 0, 2).reshape(C, KV * HD)
    new_keys = token_keys.reshape(token_count, KV * HD)
    new_values = token_values.reshape(token_count, KV * HD)
    return (attn_out, grad_key, grad_value, new_keys, new_values)
```

```python
import jax
import jax.numpy as jnp
from jax import lax
from jax.experimental import pallas as pl
from jax.experimental.pallas import tpu as pltpu
from jax.sharding import PartitionSpec as P

H = 64
KV = 8
HD = 128
C = 2048
SEQ = 64


def rotate(vectors, positions):
    half_dim = vectors.shape[-1] // 2
    frequency = jnp.exp(
        -jnp.log(500000.0) * jnp.arange(half_dim, dtype=jnp.float32) * (2.0 / vectors.shape[-1])
    )
    angles = positions.astype(jnp.float32)[:, None] * frequency[None, :]
    cosines = jnp.cos(angles)[:, None, :]
    sine_table = jnp.sin(angles)[:, None, :]
    first_half = vectors[..., :half_dim]
    second = vectors[..., half_dim:]
    return jnp.concatenate(
        [first_half * cosines - second * sine_table, second * cosines + first_half * sine_table], -1
    )


def head_block(queries, slot_keys, slot_values, token_keys, token_values, grad_heads, seq_len):
    scaling = queries.shape[-1] ** (-0.5)
    token_count = queries.shape[1]
    score_cart = (
        jnp.einsum("gtd,cd->gtc", queries, slot_keys, preferred_element_type=jnp.float32) * scaling
    )
    score_tok = (
        jnp.einsum("gtd,sd->gts", queries, token_keys, preferred_element_type=jnp.float32) * scaling
    )
    index_rows = jnp.arange(token_count)
    causal = (index_rows[:, None] // seq_len == index_rows[None, :] // seq_len) & (
        index_rows[None, :] <= index_rows[:, None]
    )
    score_tok = jnp.where(causal[None], score_tok, -jnp.inf)
    row_max = jnp.maximum(
        jnp.max(score_cart, -1, keepdims=True), jnp.max(score_tok, -1, keepdims=True)
    )
    exp_cart = jnp.exp(score_cart - row_max)
    exp_tok = jnp.exp(score_tok - row_max)
    totals = jnp.sum(exp_cart, -1, keepdims=True) + jnp.sum(exp_tok, -1, keepdims=True)
    prob_cart = exp_cart / totals
    rounded_cart = prob_cart.astype(jnp.bfloat16)
    rounded_tok = (exp_tok / totals).astype(jnp.bfloat16)
    mixture = jnp.einsum(
        "gtc,cd->gtd", rounded_cart, slot_values, preferred_element_type=jnp.float32
    )
    mixture = mixture + jnp.einsum(
        "gts,sd->gtd", rounded_tok, token_values, preferred_element_type=jnp.float32
    )
    outputs = mixture.astype(jnp.bfloat16)
    grad_prob_cart = jnp.einsum(
        "gtd,cd->gtc", grad_heads, slot_values, preferred_element_type=jnp.float32
    )
    deltas = jnp.sum(
        grad_heads.astype(jnp.float32) * outputs.astype(jnp.float32), -1, keepdims=True
    )
    grad_score = (prob_cart * (grad_prob_cart - deltas)).astype(jnp.bfloat16)
    grad_keys = (
        jnp.einsum("gtc,gtd->cd", grad_score, queries, preferred_element_type=jnp.float32) * scaling
    )
    grad_values = jnp.einsum(
        "gtc,gtd->cd", rounded_cart, grad_heads, preferred_element_type=jnp.float32
    )
    return (outputs, grad_keys, grad_values)


def on_device(
    layer_input, norm_gain, w_query, w_key, w_value, w_out, cart_key, cart_value, grad_out
):
    devices = lax.axis_size("fsdp")
    my_index = lax.axis_index("fsdp")
    token_count = layer_input.shape[0]
    feature_count = layer_input.shape[1]
    local_heads = w_query.shape[1] // HD
    slot_count = cart_key.shape[0]
    kv_width = w_key.shape[1]
    gathered, gathered_gain = (
        lax.all_gather(layer_input, "fsdp", axis=1, tiled=True),
        lax.all_gather(norm_gain, "fsdp", axis=0, tiled=True),
    )
    gathered_f32 = gathered.astype(jnp.float32)
    inverse_rms = lax.rsqrt(jnp.mean(gathered_f32 * gathered_f32, -1, keepdims=True) + 1e-05)
    normed = (gathered_f32 * inverse_rms * gathered_gain.astype(jnp.float32)[None, :]).astype(
        jnp.bfloat16
    )
    own_part = lax.dynamic_slice_in_dim(normed, my_index * feature_count, feature_count, 1)
    partial_kv = jnp.concatenate(
        [
            jnp.dot(own_part, w_key, preferred_element_type=jnp.float32),
            jnp.dot(own_part, w_value, preferred_element_type=jnp.float32),
        ],
        1,
    )
    token_kv = lax.psum(partial_kv, "fsdp")
    positions = C + jnp.arange(token_count) % SEQ
    all_token_keys = (
        rotate(token_kv[:, :kv_width].reshape(token_count, kv_width // HD, HD), positions)
        .reshape(token_count, kv_width)
        .astype(jnp.bfloat16)
    )
    all_token_values = token_kv[:, kv_width:].astype(jnp.bfloat16)
    column_count = kv_width // devices
    new_keys = lax.dynamic_slice_in_dim(all_token_keys, my_index * column_count, column_count, 1)
    new_values = lax.dynamic_slice_in_dim(
        all_token_values, my_index * column_count, column_count, 1
    )
    kv_group = my_index * local_heads // (H // KV)
    token_keys = lax.dynamic_slice_in_dim(all_token_keys, kv_group * HD, HD, 1)
    token_values = lax.dynamic_slice_in_dim(all_token_values, kv_group * HD, HD, 1)
    queries = jnp.dot(normed, w_query, preferred_element_type=jnp.float32).reshape(
        token_count, local_heads, HD
    )
    queries = rotate(queries, positions).astype(jnp.bfloat16).transpose(1, 0, 2)
    spread_keys = jnp.repeat(cart_key.reshape(slot_count, KV, HD), devices // KV, axis=1)
    spread_values = jnp.repeat(cart_value.reshape(slot_count, KV, HD), devices // KV, axis=1)
    own_slots = lax.all_to_all(
        jnp.concatenate([spread_keys, spread_values], 2),
        "fsdp",
        split_axis=1,
        concat_axis=0,
        tiled=True,
    )
    slot_keys = own_slots[:, 0, :HD]
    slot_values = own_slots[:, 0, HD:]
    cotangent = lax.all_gather(grad_out, "fsdp", axis=1, tiled=True)
    grad_heads = lax.dot_general(
        cotangent, w_out, (((1,), (1,)), ((), ())), preferred_element_type=jnp.float32
    )
    grad_heads = (
        grad_heads.astype(jnp.bfloat16).reshape(token_count, local_heads, HD).transpose(1, 0, 2)
    )
    outputs, grad_keys, grad_values = head_block(
        queries, slot_keys, slot_values, token_keys, token_values, grad_heads, SEQ
    )
    head_outputs = outputs.transpose(1, 0, 2).reshape(token_count, local_heads * HD)
    partial_out = jnp.dot(head_outputs, w_out, preferred_element_type=jnp.float32)
    attn_out = lax.psum_scatter(partial_out, "fsdp", scatter_dimension=1, tiled=True).astype(
        jnp.bfloat16
    )
    total_slots = grad_keys.shape[0]
    stacked = jnp.concatenate([grad_keys, grad_values], 1).reshape(
        devices, total_slots // devices, 2 * HD
    )
    received = lax.all_to_all(stacked, "fsdp", split_axis=0, concat_axis=0, tiled=True)
    summed = jnp.sum(
        received.reshape(KV, devices // KV, total_slots // devices, 2 * HD), axis=1
    ).transpose(1, 0, 2)
    grad_key = summed[:, :, :HD].reshape(total_slots // devices, KV * HD)
    grad_value = summed[:, :, HD:].reshape(total_slots // devices, KV * HD)
    return (attn_out, grad_key, grad_value, new_keys, new_values)


BF = jnp.bfloat16
F32 = jnp.float32
ROWS = 128


def dot(a, b):
    return jnp.dot(a, b, preferred_element_type=F32)


def dot_t(a, b):
    return lax.dot_general(a, b, (((1,), (1,)), ((), ())), preferred_element_type=F32)


def layer_kernel(
    x_ref, gain_ref, cos_ref, sin_ref, wq_hbm, wk_hbm, wv_hbm, wo_hbm, ck_ref, cv_ref, go_ref,
    out_ref, gk_ref, gv_ref, nk_ref, nv_ref,
    normed, cot, wq, wk, wv, wo, slot_k, slot_v, squares,
    kv_swap, kv_got, kv_send, kv_recv, tok,
    queries, probs, heads, grads, acc, acc_got, g_send, g_recv,
    o_swap, o_got, y_send, y_recv, z_send, z_recv,
    load_sem, sq_send, sq_recv, cart_send, cart_recv, n_send, n_recv, c_send, c_recv,
    kv_ssem, kv_rsem, os_send, os_recv, gr_send, gr_recv,
):
    me = lax.axis_index("fsdp")
    core = lax.rem(me, 2)
    chip = me // 2
    ydim = lax.rem(chip, 2)
    zdim = chip // 2
    other = 1 - core

    def device(chip_index, core_index):
        return {"fsdp": chip_index * 2 + core_index}

    def zchip(steps, yy):
        return lax.rem(zdim + steps + 4, 4) * 2 + yy

    def remote(source, target, send, recv, where):
        return pltpu.make_async_remote_copy(
            src_ref=source, dst_ref=target, send_sem=send, recv_sem=recv,
            device_id=where, device_id_type=pl.DeviceIdType.MESH,
        )

    sent = []

    def push(source, target, send, recv, where):
        copy = remote(source, target, send, recv, where)
        copy.start()
        sent.append(copy)
        return copy

    loads = [
        pltpu.make_async_copy(source, target, load_sem.at[index])
        for index, (source, target) in enumerate(
            [(wk_hbm, wk), (wv_hbm, wv), (wq_hbm, wq), (wo_hbm, wo)]
        )
    ]
    for load in loads:
        load.start()

    barrier = pltpu.get_barrier_semaphore()
    for step in range(1, 16):
        pl.semaphore_signal(
            barrier, inc=1, device_id={"fsdp": lax.rem(me + step, 16)},
            device_id_type=pl.DeviceIdType.MESH,
        )

    x = x_ref[...].astype(F32)
    own = jnp.sum(x * x, axis=1, keepdims=True)
    squares[0] = jnp.broadcast_to(own, (256, 128)).T[:8]
    pl.semaphore_wait(barrier, 15)

    sq = [
        push(squares.at[0], squares.at[step], sq_send.at[step - 1], sq_recv.at[step - 1],
             {"fsdp": lax.rem(me + step, 16)})
        for step in range(1, 16)
    ]

    cart = []
    for step in range(1, 8):
        there = lax.rem(chip + step, 8)
        columns = pl.ds(pl.multiple_of(there * 128, 128), 128)
        cart.append(push(ck_ref.at[:, columns], slot_k.at[core, chip], cart_send.at[0, step],
                         cart_recv.at[0, step], device(there, core)))
        cart.append(push(cv_ref.at[:, columns], slot_v.at[core, chip], cart_send.at[1, step],
                         cart_recv.at[1, step], device(there, core)))
    mine = pl.ds(pl.multiple_of(chip * 128, 128), 128)
    slot_k[core, chip] = ck_ref[:, mine]
    slot_v[core, chip] = cv_ref[:, mine]

    for copy in sq:
        copy.wait_recv()
    total = squares[0]
    for step in range(1, 16):
        total = total + squares[step]
    total = jnp.broadcast_to(total[:1], (128, 256)).T[:, :1]
    inverse = lax.rsqrt(total * (1.0 / 8192.0) + 1e-05)
    normed[core, chip] = (
        x_ref[...].astype(F32) * inverse * gain_ref[...].astype(F32)
    ).astype(BF)
    cot[core, chip] = go_ref[...]

    def gather_start(buffer, k):
        own_slot = buffer.at[core, chip]
        first = [
            push(own_slot, own_slot, n_send.at[k, 0, d], n_recv.at[k, 0, d], device(zchip(d, ydim), core))
            for d in range(1, 4)
        ]
        second = [push(own_slot, own_slot, n_send.at[k, 1, 0], n_recv.at[k, 1, 0], device(zdim * 2 + 1 - ydim, core))]
        push(own_slot, own_slot, c_send.at[k, 0, 0], c_recv.at[k, 0, 0], device(chip, other))
        return first, second

    def gather_forward(buffer, k, first, second):
        for d in range(1, 4):
            first[d - 1].wait_recv()
            slot = buffer.at[core, zchip(-d, ydim)]
            second.append(push(slot, slot, n_send.at[k, 1, d], n_recv.at[k, 1, d], device(zdim * 2 + 1 - ydim, core)))
            push(slot, slot, c_send.at[k, 0, d], c_recv.at[k, 0, d], device(chip, other))

    def gather_finish(buffer, k, second):
        for d in range(4):
            second[d].wait_recv()
            slot = buffer.at[core, zchip(-d, 1 - ydim)]
            push(slot, slot, c_send.at[k, 1, d], c_recv.at[k, 1, d], device(chip, other))
        for part in range(2):
            for d in range(4):
                slot = buffer.at[other, zchip(-d, ydim if part == 0 else 1 - ydim)]
                remote(slot, slot, c_send.at[k, part, d], c_recv.at[k, part, d], device(chip, other)).wait_recv()

    first_n, second_n = gather_start(normed, 0)

    loads[0].wait()
    loads[1].wait()

    def partial_kv(g, tokens_of):
        rows = pl.ds(pl.multiple_of(tokens_of * ROWS, ROWS), ROWS)
        columns = pl.ds(pl.multiple_of(g * 128, 128), 128)
        left = normed[core, chip, rows, :]
        return dot(left, wk[:, columns]), dot(left, wv[:, columns])

    @pl.loop(0, 8)
    def _(g):
        a, b = partial_kv(g, other)
        kv_swap[g, 0] = a
        kv_swap[g, 1] = b

    swap = push(kv_swap, kv_got, kv_ssem.at[0], kv_rsem.at[0], device(chip, other))
    gather_forward(normed, 0, first_n, second_n)
    swap.wait_recv()

    @pl.loop(0, 8)
    def _(g):
        a, b = partial_kv(g, core)
        kv_send[g, 0] = a + kv_got[g, 0]
        kv_send[g, 1] = b + kv_got[g, 1]

    kv = []
    for step in range(1, 8):
        there = lax.rem(chip + step, 8)
        kv.append(push(kv_send.at[there], kv_recv.at[step - 1], kv_ssem.at[step], kv_rsem.at[step], device(there, core)))
    gather_finish(normed, 0, second_n)
    first_g, second_g = gather_start(cot, 1)

    loads[2].wait()

    def project(source, weight):
        def body(index, total):
            cc, g = index // 8, lax.rem(index, 8)
            rows = pl.ds(pl.multiple_of((g * 2 + cc) * 512, 512), 512)
            return total + dot(source[cc, g], weight[rows, :])
        return lax.fori_loop(0, 16, body, jnp.zeros((256, 512), F32))

    cosines = cos_ref[...]
    sines = sin_ref[...]

    def rotated(v, c, s):
        return v * c + pltpu.roll(v, 64, 1) * s

    cos2 = jnp.concatenate([cosines, cosines], 0)
    sin2 = jnp.concatenate([sines, sines], 0)
    q_all = project(normed, wq)
    for h in range(4):
        queries[h] = rotated(q_all[:, h * 128:(h + 1) * 128], cos2, sin2).astype(BF)

    for copy in cart:
        copy.wait_recv()
    swap_k = push(slot_k.at[core], slot_k.at[core], cart_send.at[0, 0], cart_recv.at[0, 0], device(chip, other))
    swap_v = push(slot_v.at[core], slot_v.at[core], cart_send.at[1, 0], cart_recv.at[1, 0], device(chip, other))
    for copy in kv:
        copy.wait_recv()
    key_sum = kv_send[chip, 0]
    value_sum = kv_send[chip, 1]
    for step in range(7):
        key_sum = key_sum + kv_recv[step, 0]
        value_sum = value_sum + kv_recv[step, 1]
    tok[core, 0] = rotated(key_sum, cosines, sines).astype(BF)
    tok[core, 1] = value_sum.astype(BF)
    swap_t = push(tok.at[core], tok.at[core], kv_ssem.at[8], kv_rsem.at[8], device(chip, other))
    gather_forward(cot, 1, first_g, second_g)
    swap_t.wait_recv()
    for half in range(2):
        rows = slice(half * ROWS, (half + 1) * ROWS)
        for which, target in ((0, nk_ref), (1, nv_ref)):
            block = tok[half, which].astype(F32)
            target[rows, :] = jnp.where(core == 0, block[:, :64], block[:, 64:]).astype(BF)
    swap_k.wait_recv()
    swap_v.wait_recv()

    scaling = HD ** (-0.5)
    token_row = lax.broadcasted_iota(jnp.int32, (ROWS, ROWS), 0)
    token_col = lax.broadcasted_iota(jnp.int32, (ROWS, ROWS), 1)
    causal = (token_row // SEQ == token_col // SEQ) & (token_col <= token_row)

    @pl.loop(0, 8)
    def _(index):
        h, half = index // 2, lax.rem(index, 2)
        rows = pl.ds(pl.multiple_of(half * ROWS, ROWS), ROWS)
        q = queries[h, rows, :]
        keys = slot_k[...].reshape(C, HD)
        score = dot_t(q, keys) * scaling
        score_tok = jnp.where(causal, dot_t(q, tok[half, 0]) * scaling, -jnp.inf)
        top = jnp.maximum(
            jnp.max(score, -1, keepdims=True), jnp.max(score_tok, -1, keepdims=True)
        )
        e = jnp.exp(score - top)
        e_tok = jnp.exp(score_tok - top)
        inv = 1.0 / (jnp.sum(e, -1, keepdims=True) + jnp.sum(e_tok, -1, keepdims=True))
        p = e * inv
        probs[h, rows, :] = p
        mixture = dot(p.astype(BF), slot_v[...].reshape(C, HD))
        mixture = mixture + dot((e_tok * inv).astype(BF), tok[half, 1])
        heads[h, rows, :] = mixture.astype(BF)

    gather_finish(cot, 1, second_g)

    loads[3].wait()
    all_heads = jnp.concatenate([heads[h] for h in range(4)], 1)

    def partial_out(g, cc):
        columns = pl.ds(pl.multiple_of((g * 2 + cc) * 512, 512), 512)
        return dot(all_heads, wo[:, columns])

    swaps = []
    for index, (d, yy) in enumerate([(d, k) for k in (1, 0) for d in (1, 2, 3, 0)]):
        g = zchip(d, 1 - ydim if yy else ydim)
        o_swap[index] = partial_out(g, other)
        swaps.append(push(o_swap.at[index], o_got.at[index], os_send.at[0, index], os_recv.at[0, index], device(chip, other)))
    ys = []
    for index, d in enumerate((1, 2, 3, 0)):
        part = partial_out(zchip(d, 1 - ydim), core)
        swaps[index].wait_recv()
        y_send[index] = (part + o_got[index]).astype(BF)
        ys.append(push(y_send.at[index], y_recv.at[index], os_send.at[1, index], os_recv.at[1, index], device(zdim * 2 + 1 - ydim, core)))

    def grad_body(index, total):
        cc, g = index // 8, lax.rem(index, 8)
        columns = pl.ds(pl.multiple_of((g * 2 + cc) * 512, 512), 512)
        return total + dot_t(cot[cc, g], wo[:, columns])

    g_all = lax.fori_loop(0, 16, grad_body, jnp.zeros((256, 512), F32)).astype(BF)
    for h in range(4):
        grads[h] = g_all[:, h * 128:(h + 1) * 128]

    zs = []
    for index, d in enumerate((1, 2, 3)):
        part = partial_out(zchip(d, ydim), core)
        swaps[4 + index].wait_recv()
        ys[index].wait_recv()
        z_send[index] = (part + o_got[4 + index] + y_recv[index].astype(F32)).astype(BF)
        zs.append(push(z_send.at[index], z_recv.at[index], os_send.at[2, index], os_recv.at[2, index], device(zchip(d, ydim), core)))

    acc[...] = jnp.zeros_like(acc)

    @pl.loop(0, 8)
    def _(index):
        h, half = index // 2, lax.rem(index, 2)
        rows = pl.ds(pl.multiple_of(half * ROWS, ROWS), ROWS)
        q_t = queries[h, rows, :].T
        gh = grads[h, rows, :]
        gh_t = gh.T
        delta = jnp.sum(gh.astype(F32) * heads[h, rows, :].astype(F32), -1, keepdims=True)
        for cc in range(2):
            values = slot_v[cc].reshape(C // 2, HD)
            p = probs[h, rows, cc * (C // 2):(cc + 1) * (C // 2)]
            score = (p * (dot_t(gh, values) - delta)).astype(BF)
            acc[cc, 0] += dot(q_t, score)
            acc[cc, 1] += dot(gh_t, p.astype(BF))

    swap_a = push(acc.at[other], acc_got, gr_send.at[0], gr_recv.at[0], device(chip, other))

    part = partial_out(chip, core)
    swaps[7].wait_recv()
    ys[3].wait_recv()
    part = part + o_got[7] + y_recv[3].astype(F32)
    for index in range(3):
        zs[index].wait_recv()
        part = part + z_recv[index].astype(F32)
    out_ref[...] = part.astype(BF)

    swap_a.wait_recv()
    for which in range(2):
        both = acc[core, which] + acc_got[which]
        if which == 0:
            both = both * scaling
        for g in range(8):
            g_send[g, which] = both[:, g * 128:(g + 1) * 128].astype(BF)
    gs = []
    for step in range(1, 8):
        there = lax.rem(chip + step, 8)
        gs.append(push(g_send.at[there], g_recv.at[step - 1], gr_send.at[step], gr_recv.at[step], device(there, core)))

    gk_ref[:, mine] = g_send[chip, 0].astype(F32).T
    gv_ref[:, mine] = g_send[chip, 1].astype(F32).T
    for step in range(1, 8):
        gs[step - 1].wait_recv()
        columns = pl.ds(pl.multiple_of(lax.rem(chip - step + 8, 8) * 128, 128), 128)
        gk_ref[:, columns] = g_recv[step - 1, 0].astype(F32).T
        gv_ref[:, columns] = g_recv[step - 1, 1].astype(F32).T
    for copy in sent:
        copy.wait_send()


def on_chip_grid(
    layer_input, norm_gain, w_query, w_key, w_value, w_out, cart_key, cart_value, grad_out
):
    half = HD // 2
    frequency = jnp.exp(-jnp.log(500000.0) * jnp.arange(half, dtype=F32) * (2.0 / HD))
    positions = C + jnp.arange(ROWS) % SEQ
    angles = positions.astype(F32)[:, None] * frequency[None, :]
    cosines = jnp.concatenate([jnp.cos(angles), jnp.cos(angles)], 1)
    sines = jnp.concatenate([-jnp.sin(angles), jnp.sin(angles)], 1)
    vmem = pl.BlockSpec(memory_space=pltpu.VMEM)
    hbm = pl.BlockSpec(memory_space=pl.ANY)
    V = pltpu.VMEM
    dma = pltpu.SemaphoreType.DMA
    return tuple(pl.pallas_call(
        layer_kernel,
        out_shape=(
            jax.ShapeDtypeStruct((256, 512), BF),
            jax.ShapeDtypeStruct((128, 1024), F32),
            jax.ShapeDtypeStruct((128, 1024), F32),
            jax.ShapeDtypeStruct((256, 64), BF),
            jax.ShapeDtypeStruct((256, 64), BF),
        ),
        in_specs=[vmem, vmem, vmem, vmem, hbm, hbm, hbm, hbm, vmem, vmem, vmem],
        out_specs=(vmem,) * 5,
        scratch_shapes=[
            V((2, 8, 256, 512), BF), V((2, 8, 256, 512), BF),
            V((8192, 512), BF), V((512, 1024), BF), V((512, 1024), BF), V((512, 8192), BF),
            V((2, 8, 128, 128), BF), V((2, 8, 128, 128), BF), V((16, 8, 256), F32),
            V((8, 2, 128, 128), F32), V((8, 2, 128, 128), F32), V((8, 2, 128, 128), F32),
            V((7, 2, 128, 128), F32), V((2, 2, 128, 128), BF),
            V((4, 256, 128), BF), V((4, 256, 2048), F32), V((4, 256, 128), BF), V((4, 256, 128), BF),
            V((2, 2, 128, 1024), F32), V((2, 128, 1024), F32),
            V((8, 2, 128, 128), BF), V((7, 2, 128, 128), BF),
            V((8, 256, 512), F32), V((8, 256, 512), F32),
            V((4, 256, 512), BF), V((4, 256, 512), BF), V((3, 256, 512), BF), V((3, 256, 512), BF),
            dma((4,)), dma((15,)), dma((15,)), dma((2, 8)), dma((2, 8)),
            dma((2, 2, 4)), dma((2, 2, 4)), dma((2, 2, 4)), dma((2, 2, 4)),
            dma((9,)), dma((9,)), dma((3, 8)), dma((3, 8)), dma((8,)), dma((8,)),
        ],
        compiler_params=pltpu.CompilerParams(
            collective_id=0, has_side_effects=True, vmem_limit_bytes=63 * 2**20
        ),
        name="attention_layer",
    )(
        layer_input, norm_gain.reshape(1, -1), cosines, sines, w_query, w_key, w_value, w_out,
        cart_key, cart_value, grad_out,
    ))


def solution(mesh):
    body = on_chip_grid if mesh.shape["fsdp"] == 16 else on_device
    return jax.shard_map(
        body,
        mesh=mesh,
        in_specs=(
            P("groups", "fsdp"),
            P("fsdp"),
            P(None, "fsdp"),
            P("fsdp", None),
            P("fsdp", None),
            P("fsdp", None),
            P(("groups", "fsdp"), None),
            P(("groups", "fsdp"), None),
            P("groups", "fsdp"),
        ),
        out_specs=(
            P("groups", "fsdp"),
            P(("groups", "fsdp"), None),
            P(("groups", "fsdp"), None),
            P("groups", "fsdp"),
            P("groups", "fsdp"),
        ),
        check_vma=False,
    )
```

```python
import jax
import jax.numpy as jnp
from jax import lax
from jax.experimental import pallas as pl
from jax.experimental.pallas import tpu as pltpu
from jax.sharding import PartitionSpec as P

H = 64
KV = 8
HD = 128
C = 2048
SEQ = 64


def rotate(vectors, positions):
    half_dim = vectors.shape[-1] // 2
    frequency = jnp.exp(
        -jnp.log(500000.0) * jnp.arange(half_dim, dtype=jnp.float32) * (2.0 / vectors.shape[-1])
    )
    angles = positions.astype(jnp.float32)[:, None] * frequency[None, :]
    cosines = jnp.cos(angles)[:, None, :]
    sine_table = jnp.sin(angles)[:, None, :]
    first_half = vectors[..., :half_dim]
    second = vectors[..., half_dim:]
    return jnp.concatenate(
        [first_half * cosines - second * sine_table, second * cosines + first_half * sine_table], -1
    )


def head_block(queries, slot_keys, slot_values, token_keys, token_values, grad_heads, seq_len):
    scaling = queries.shape[-1] ** (-0.5)
    token_count = queries.shape[1]
    score_cart = (
        jnp.einsum("gtd,cd->gtc", queries, slot_keys, preferred_element_type=jnp.float32) * scaling
    )
    score_tok = (
        jnp.einsum("gtd,sd->gts", queries, token_keys, preferred_element_type=jnp.float32) * scaling
    )
    index_rows = jnp.arange(token_count)
    causal = (index_rows[:, None] // seq_len == index_rows[None, :] // seq_len) & (
        index_rows[None, :] <= index_rows[:, None]
    )
    score_tok = jnp.where(causal[None], score_tok, -jnp.inf)
    row_max = jnp.maximum(
        jnp.max(score_cart, -1, keepdims=True), jnp.max(score_tok, -1, keepdims=True)
    )
    exp_cart = jnp.exp(score_cart - row_max)
    exp_tok = jnp.exp(score_tok - row_max)
    totals = jnp.sum(exp_cart, -1, keepdims=True) + jnp.sum(exp_tok, -1, keepdims=True)
    prob_cart = exp_cart / totals
    rounded_cart = prob_cart.astype(jnp.bfloat16)
    rounded_tok = (exp_tok / totals).astype(jnp.bfloat16)
    mixture = jnp.einsum(
        "gtc,cd->gtd", rounded_cart, slot_values, preferred_element_type=jnp.float32
    )
    mixture = mixture + jnp.einsum(
        "gts,sd->gtd", rounded_tok, token_values, preferred_element_type=jnp.float32
    )
    outputs = mixture.astype(jnp.bfloat16)
    grad_prob_cart = jnp.einsum(
        "gtd,cd->gtc", grad_heads, slot_values, preferred_element_type=jnp.float32
    )
    deltas = jnp.sum(
        grad_heads.astype(jnp.float32) * outputs.astype(jnp.float32), -1, keepdims=True
    )
    grad_score = (prob_cart * (grad_prob_cart - deltas)).astype(jnp.bfloat16)
    grad_keys = (
        jnp.einsum("gtc,gtd->cd", grad_score, queries, preferred_element_type=jnp.float32) * scaling
    )
    grad_values = jnp.einsum(
        "gtc,gtd->cd", rounded_cart, grad_heads, preferred_element_type=jnp.float32
    )
    return (outputs, grad_keys, grad_values)


def on_device(
    layer_input, norm_gain, w_query, w_key, w_value, w_out, cart_key, cart_value, grad_out
):
    devices = lax.axis_size("fsdp")
    my_index = lax.axis_index("fsdp")
    token_count = layer_input.shape[0]
    feature_count = layer_input.shape[1]
    local_heads = w_query.shape[1] // HD
    slot_count = cart_key.shape[0]
    kv_width = w_key.shape[1]
    gathered, gathered_gain = (
        lax.all_gather(layer_input, "fsdp", axis=1, tiled=True),
        lax.all_gather(norm_gain, "fsdp", axis=0, tiled=True),
    )
    gathered_f32 = gathered.astype(jnp.float32)
    inverse_rms = lax.rsqrt(jnp.mean(gathered_f32 * gathered_f32, -1, keepdims=True) + 1e-05)
    normed = (gathered_f32 * inverse_rms * gathered_gain.astype(jnp.float32)[None, :]).astype(
        jnp.bfloat16
    )
    own_part = lax.dynamic_slice_in_dim(normed, my_index * feature_count, feature_count, 1)
    partial_kv = jnp.concatenate(
        [
            jnp.dot(own_part, w_key, preferred_element_type=jnp.float32),
            jnp.dot(own_part, w_value, preferred_element_type=jnp.float32),
        ],
        1,
    )
    token_kv = lax.psum(partial_kv, "fsdp")
    positions = C + jnp.arange(token_count) % SEQ
    all_token_keys = (
        rotate(token_kv[:, :kv_width].reshape(token_count, kv_width // HD, HD), positions)
        .reshape(token_count, kv_width)
        .astype(jnp.bfloat16)
    )
    all_token_values = token_kv[:, kv_width:].astype(jnp.bfloat16)
    column_count = kv_width // devices
    new_keys = lax.dynamic_slice_in_dim(all_token_keys, my_index * column_count, column_count, 1)
    new_values = lax.dynamic_slice_in_dim(
        all_token_values, my_index * column_count, column_count, 1
    )
    kv_group = my_index * local_heads // (H // KV)
    token_keys = lax.dynamic_slice_in_dim(all_token_keys, kv_group * HD, HD, 1)
    token_values = lax.dynamic_slice_in_dim(all_token_values, kv_group * HD, HD, 1)
    queries = jnp.dot(normed, w_query, preferred_element_type=jnp.float32).reshape(
        token_count, local_heads, HD
    )
    queries = rotate(queries, positions).astype(jnp.bfloat16).transpose(1, 0, 2)
    spread_keys = jnp.repeat(cart_key.reshape(slot_count, KV, HD), devices // KV, axis=1)
    spread_values = jnp.repeat(cart_value.reshape(slot_count, KV, HD), devices // KV, axis=1)
    own_slots = lax.all_to_all(
        jnp.concatenate([spread_keys, spread_values], 2),
        "fsdp",
        split_axis=1,
        concat_axis=0,
        tiled=True,
    )
    slot_keys = own_slots[:, 0, :HD]
    slot_values = own_slots[:, 0, HD:]
    cotangent = lax.all_gather(grad_out, "fsdp", axis=1, tiled=True)
    grad_heads = lax.dot_general(
        cotangent, w_out, (((1,), (1,)), ((), ())), preferred_element_type=jnp.float32
    )
    grad_heads = (
        grad_heads.astype(jnp.bfloat16).reshape(token_count, local_heads, HD).transpose(1, 0, 2)
    )
    outputs, grad_keys, grad_values = head_block(
        queries, slot_keys, slot_values, token_keys, token_values, grad_heads, SEQ
    )
    head_outputs = outputs.transpose(1, 0, 2).reshape(token_count, local_heads * HD)
    partial_out = jnp.dot(head_outputs, w_out, preferred_element_type=jnp.float32)
    attn_out = lax.psum_scatter(partial_out, "fsdp", scatter_dimension=1, tiled=True).astype(
        jnp.bfloat16
    )
    total_slots = grad_keys.shape[0]
    stacked = jnp.concatenate([grad_keys, grad_values], 1).reshape(
        devices, total_slots // devices, 2 * HD
    )
    received = lax.all_to_all(stacked, "fsdp", split_axis=0, concat_axis=0, tiled=True)
    summed = jnp.sum(
        received.reshape(KV, devices // KV, total_slots // devices, 2 * HD), axis=1
    ).transpose(1, 0, 2)
    grad_key = summed[:, :, :HD].reshape(total_slots // devices, KV * HD)
    grad_value = summed[:, :, HD:].reshape(total_slots // devices, KV * HD)
    return (attn_out, grad_key, grad_value, new_keys, new_values)


BF = jnp.bfloat16
F32 = jnp.float32
ROWS = 128


def dot(a, b):
    return jnp.dot(a, b, preferred_element_type=F32)


def dot_t(a, b):
    return lax.dot_general(a, b, (((1,), (1,)), ((), ())), preferred_element_type=F32)


def layer_kernel(
    x_ref, gain_ref, cos_ref, sin_ref, wq_hbm, wk_hbm, wv_hbm, wo_hbm, ck_ref, cv_ref, go_ref,
    out_ref, gk_ref, gv_ref, nk_ref, nv_ref,
    normed, cot, wq, wk, wv, wo, slot_k, slot_v, squares,
    kv_swap, kv_got, kv_send, kv_y, kv_z, kv_recv, tok,
    queries, probs, heads, grads, acc, acc_got, g_send, g_recv,
    o_swap, o_got, y_send, y_recv, z_send, z_recv,
    load_sem, sq_send, sq_recv, cart_send, cart_recv, n_send, n_recv, yg_send, yg_recv, c_send, c_recv,
    kv_ssem, kv_rsem, os_send, os_recv, gr_send, gr_recv,
):
    me = lax.axis_index("fsdp")
    core = lax.rem(me, 2)
    chip = me // 2
    ydim = lax.rem(chip, 2)
    zdim = chip // 2
    other = 1 - core

    def device(chip_index, core_index):
        return {"fsdp": chip_index * 2 + core_index}

    def zchip(steps, yy):
        return lax.rem(zdim + steps + 4, 4) * 2 + yy

    def remote(source, target, send, recv, where):
        return pltpu.make_async_remote_copy(
            src_ref=source, dst_ref=target, send_sem=send, recv_sem=recv,
            device_id=where, device_id_type=pl.DeviceIdType.MESH,
        )

    sent = []

    def guarded(valid, action):
        if valid is None:
            action()
        else:
            pl.when(valid)(action)

    def push(source, target, send, recv, where, valid=None):
        copy = remote(source, target, send, recv, where)
        guarded(valid, copy.start)
        sent.append((valid, copy))
        return copy

    loads = [
        pltpu.make_async_copy(source, target, load_sem.at[index])
        for index, (source, target) in enumerate(
            [(wk_hbm, wk), (wv_hbm, wv), (wq_hbm, wq), (wo_hbm, wo)]
        )
    ]
    for load in loads:
        load.start()

    barrier = pltpu.get_barrier_semaphore()
    for step in range(1, 16):
        pl.semaphore_signal(
            barrier, inc=1, device_id={"fsdp": lax.rem(me + step, 16)},
            device_id_type=pl.DeviceIdType.MESH,
        )

    x = x_ref[...].astype(F32)
    own = jnp.sum(x * x, axis=1, keepdims=True)
    squares[0] = jnp.broadcast_to(own, (256, 128)).T[:8]
    pl.semaphore_wait(barrier, 15)

    sq = [
        push(squares.at[0], squares.at[step], sq_send.at[step - 1], sq_recv.at[step - 1],
             {"fsdp": lax.rem(me + step, 16)})
        for step in range(1, 16)
    ]

    cart = []
    for step in range(1, 8):
        there = lax.rem(chip + step, 8)
        columns = pl.ds(pl.multiple_of(there * 128, 128), 128)
        cart.append(push(ck_ref.at[:, columns], slot_k.at[core, chip], cart_send.at[0, step],
                         cart_recv.at[0, step], device(there, core)))
        cart.append(push(cv_ref.at[:, columns], slot_v.at[core, chip], cart_send.at[1, step],
                         cart_recv.at[1, step], device(there, core)))
    mine = pl.ds(pl.multiple_of(chip * 128, 128), 128)
    slot_k[core, chip] = ck_ref[:, mine]
    slot_v[core, chip] = cv_ref[:, mine]

    for copy in sq:
        copy.wait_recv()
    total = squares[0]
    for step in range(1, 16):
        total = total + squares[step]
    total = jnp.broadcast_to(total[:1], (128, 256)).T[:, :1]
    inverse = lax.rsqrt(total * (1.0 / 8192.0) + 1e-05)
    normed[core, chip] = (
        x_ref[...].astype(F32) * inverse * gain_ref[...].astype(F32)
    ).astype(BF)
    cot[core, chip] = go_ref[...]

    above = device(zchip(1, ydim), core)
    below = device(zchip(-1, ydim), core)
    across = device(zdim * 2 + 1 - ydim, core)
    twin = device(chip, other)

    def arrivals(step):
        return (
            (0, -1 - step, zdim >= 1 + step, (zdim >= 1 + step) & (zdim < 3), above),
            (1, 1 + step, zdim < 3 - step, (zdim < 3 - step) & (zdim > 0), below),
        )

    def gather_start(buffer, k):
        slot = buffer.at[core, chip]
        push(slot, slot, n_send.at[k, 0, 0], n_recv.at[k, 0, 0], above, zdim < 3)
        push(slot, slot, n_send.at[k, 1, 0], n_recv.at[k, 1, 0], below, zdim > 0)
        push(slot, slot, yg_send.at[k, 6], yg_recv.at[k, 6], across)
        push(slot, slot, c_send.at[k, 0, 6], c_recv.at[k, 0, 6], twin)

    def gather_step(buffer, k, step):
        for way, offset, here, further, onward in arrivals(step):
            slot = buffer.at[core, zchip(offset, ydim)]
            number = way * 3 + step
            arrived = remote(slot, slot, n_send.at[k, way, step], n_recv.at[k, way, step], onward)
            guarded(here, arrived.wait_recv)
            if step < 2:
                push(slot, slot, n_send.at[k, way, step + 1], n_recv.at[k, way, step + 1], onward, further)
            push(slot, slot, yg_send.at[k, number], yg_recv.at[k, number], across, here)
            push(slot, slot, c_send.at[k, 0, number], c_recv.at[k, 0, number], twin, here)

    def gather_across(buffer, k, steps):
        for step in steps:
            pairs = [(6, 0, None)] if step < 0 else [
                (way * 3 + step, offset, here) for way, offset, here, _, _ in arrivals(step)
            ]
            for number, offset, here in pairs:
                slot = buffer.at[core, zchip(offset, 1 - ydim)]
                arrived = remote(slot, slot, yg_send.at[k, number], yg_recv.at[k, number], across)
                guarded(here, arrived.wait_recv)
                push(slot, slot, c_send.at[k, 1, number], c_recv.at[k, 1, number], twin, here)

    def gather_finish(buffer, k):
        for step in (-1, 0, 1, 2):
            pairs = [(6, 0, None)] if step < 0 else [
                (way * 3 + step, offset, here) for way, offset, here, _, _ in arrivals(step)
            ]
            for number, offset, here in pairs:
                for part in range(2):
                    slot = buffer.at[other, zchip(offset, ydim if part == 0 else 1 - ydim)]
                    arrived = remote(slot, slot, c_send.at[k, part, number], c_recv.at[k, part, number], twin)
                    guarded(here, arrived.wait_recv)

    gather_start(normed, 0)

    loads[0].wait()
    loads[1].wait()

    def partial_kv(g, tokens_of):
        rows = pl.ds(pl.multiple_of(tokens_of * ROWS, ROWS), ROWS)
        columns = pl.ds(pl.multiple_of(g * 128, 128), 128)
        left = normed[core, chip, rows, :]
        return dot(left, wk[:, columns]), dot(left, wv[:, columns])

    @pl.loop(0, 8)
    def _(g):
        a, b = partial_kv(g, other)
        kv_swap[g, 0] = a
        kv_swap[g, 1] = b

    swap = push(kv_swap, kv_got, kv_ssem.at[0], kv_rsem.at[0], device(chip, other))
    gather_step(normed, 0, 0)
    swap.wait_recv()

    @pl.loop(0, 8)
    def _(g):
        a, b = partial_kv(g, core)
        yy, zz = lax.rem(g, 2), g // 2
        kv_send[yy, zz, 0] = a + kv_got[g, 0]
        kv_send[yy, zz, 1] = b + kv_got[g, 1]

    kv_across = push(kv_send.at[1 - ydim], kv_y, kv_ssem.at[1], kv_rsem.at[1], across)
    gather_step(normed, 0, 1)
    gather_across(normed, 0, (-1, 0))
    kv_across.wait_recv()
    kv = []
    for d in (1, 2, 3, 0):
        zz = lax.rem(zdim + d, 4)
        kv_z[d] = kv_send[ydim, zz] + kv_y[zz]
        if d:
            kv.append(push(kv_z.at[d], kv_recv.at[d - 1], kv_ssem.at[1 + d], kv_rsem.at[1 + d], device(zchip(d, ydim), core)))
    gather_step(normed, 0, 2)
    gather_start(cot, 1)
    gather_across(normed, 0, (1, 2))
    gather_finish(normed, 0)

    loads[2].wait()

    def project(source, weight):
        def body(index, total):
            cc, g = index // 8, lax.rem(index, 8)
            rows = pl.ds(pl.multiple_of((g * 2 + cc) * 512, 512), 512)
            return total + dot(source[cc, g], weight[rows, :])
        return lax.fori_loop(0, 16, body, jnp.zeros((256, 512), F32))

    cosines = cos_ref[...]
    sines = sin_ref[...]

    def rotated(v, c, s):
        return v * c + pltpu.roll(v, 64, 1) * s

    cos2 = jnp.concatenate([cosines, cosines], 0)
    sin2 = jnp.concatenate([sines, sines], 0)
    q_all = project(normed, wq)
    for h in range(4):
        queries[h] = rotated(q_all[:, h * 128:(h + 1) * 128], cos2, sin2).astype(BF)

    for copy in cart:
        copy.wait_recv()
    swap_k = push(slot_k.at[core], slot_k.at[core], cart_send.at[0, 0], cart_recv.at[0, 0], device(chip, other))
    swap_v = push(slot_v.at[core], slot_v.at[core], cart_send.at[1, 0], cart_recv.at[1, 0], device(chip, other))
    for copy in kv:
        copy.wait_recv()
    key_sum = kv_z[0, 0]
    value_sum = kv_z[0, 1]
    for step in range(3):
        key_sum = key_sum + kv_recv[step, 0]
        value_sum = value_sum + kv_recv[step, 1]
    tok[core, 0] = rotated(key_sum, cosines, sines).astype(BF)
    tok[core, 1] = value_sum.astype(BF)
    swap_t = push(tok.at[core], tok.at[core], kv_ssem.at[8], kv_rsem.at[8], device(chip, other))
    gather_step(cot, 1, 0)
    swap_t.wait_recv()
    for half in range(2):
        tokens = slice(half * ROWS, (half + 1) * ROWS)
        for which, target in ((0, nk_ref), (1, nv_ref)):
            block = tok[half, which].astype(F32).T
            target[:, tokens] = jnp.where(core == 0, block[:64], block[64:]).astype(BF)
    swap_k.wait_recv()
    swap_v.wait_recv()

    scaling = HD ** (-0.5)
    token_row = lax.broadcasted_iota(jnp.int32, (ROWS, ROWS), 0)
    token_col = lax.broadcasted_iota(jnp.int32, (ROWS, ROWS), 1)
    causal = (token_row // SEQ == token_col // SEQ) & (token_col <= token_row)

    def attend(index):
        h, half = index // 2, lax.rem(index, 2)
        rows = pl.ds(pl.multiple_of(half * ROWS, ROWS), ROWS)
        q = queries[h, rows, :]
        keys = slot_k[...].reshape(C, HD)
        score = dot_t(q, keys) * scaling
        score_tok = jnp.where(causal, dot_t(q, tok[half, 0]) * scaling, -jnp.inf)
        top = jnp.maximum(
            jnp.max(score, -1, keepdims=True), jnp.max(score_tok, -1, keepdims=True)
        )
        e = jnp.exp(score - top)
        e_tok = jnp.exp(score_tok - top)
        inv = 1.0 / (jnp.sum(e, -1, keepdims=True) + jnp.sum(e_tok, -1, keepdims=True))
        p = e * inv
        probs[h, rows, :] = p
        mixture = dot(p.astype(BF), slot_v[...].reshape(C, HD))
        mixture = mixture + dot((e_tok * inv).astype(BF), tok[half, 1])
        heads[h, rows, :] = mixture.astype(BF)

    pl.loop(0, 2)(attend)
    gather_step(cot, 1, 1)
    pl.loop(2, 4)(attend)
    gather_step(cot, 1, 2)
    pl.loop(4, 6)(attend)
    gather_across(cot, 1, (-1, 0))
    pl.loop(6, 8)(attend)
    gather_across(cot, 1, (1, 2))

    loads[3].wait()
    all_heads = jnp.concatenate([heads[h] for h in range(4)], 1)

    def partial_out(g, cc):
        columns = pl.ds(pl.multiple_of((g * 2 + cc) * 512, 512), 512)
        return dot(all_heads, wo[:, columns])

    swaps = []
    for index, (d, yy) in enumerate([(d, k) for k in (1, 0) for d in (1, 2, 3, 0)]):
        g = zchip(d, 1 - ydim if yy else ydim)
        o_swap[index] = partial_out(g, other)
        swaps.append(push(o_swap.at[index], o_got.at[index], os_send.at[0, index], os_recv.at[0, index], device(chip, other)))
    ys = []
    for index, d in enumerate((1, 2, 3, 0)):
        part = partial_out(zchip(d, 1 - ydim), core)
        swaps[index].wait_recv()
        y_send[index] = (part + o_got[index]).astype(BF)
        ys.append(push(y_send.at[index], y_recv.at[index], os_send.at[1, index], os_recv.at[1, index], device(zdim * 2 + 1 - ydim, core)))

    gather_finish(cot, 1)

    def grad_body(index, total):
        cc, g = index // 8, lax.rem(index, 8)
        columns = pl.ds(pl.multiple_of((g * 2 + cc) * 512, 512), 512)
        return total + dot_t(cot[cc, g], wo[:, columns])

    g_all = lax.fori_loop(0, 16, grad_body, jnp.zeros((256, 512), F32)).astype(BF)
    for h in range(4):
        grads[h] = g_all[:, h * 128:(h + 1) * 128]

    zs = []
    for index, d in enumerate((1, 2, 3)):
        part = partial_out(zchip(d, ydim), core)
        swaps[4 + index].wait_recv()
        ys[index].wait_recv()
        z_send[index] = (part + o_got[4 + index] + y_recv[index].astype(F32)).astype(BF)
        zs.append(push(z_send.at[index], z_recv.at[index], os_send.at[2, index], os_recv.at[2, index], device(zchip(d, ydim), core)))

    acc[...] = jnp.zeros_like(acc)

    @pl.loop(0, 8)
    def _(index):
        h, half = index // 2, lax.rem(index, 2)
        rows = pl.ds(pl.multiple_of(half * ROWS, ROWS), ROWS)
        q_t = queries[h, rows, :].T
        gh = grads[h, rows, :]
        gh_t = gh.T
        delta = jnp.sum(gh.astype(F32) * heads[h, rows, :].astype(F32), -1, keepdims=True)
        for cc in range(2):
            values = slot_v[cc].reshape(C // 2, HD)
            p = probs[h, rows, cc * (C // 2):(cc + 1) * (C // 2)]
            score = (p * (dot_t(gh, values) - delta)).astype(BF)
            acc[cc, 0] += dot(q_t, score)
            acc[cc, 1] += dot(gh_t, p.astype(BF))

    swap_a = push(acc.at[other], acc_got, gr_send.at[0], gr_recv.at[0], device(chip, other))

    part = partial_out(chip, core)
    swaps[7].wait_recv()
    ys[3].wait_recv()
    part = part + o_got[7] + y_recv[3].astype(F32)
    for index in range(3):
        zs[index].wait_recv()
        part = part + z_recv[index].astype(F32)
    out_ref[...] = part.astype(BF)

    swap_a.wait_recv()
    for which in range(2):
        both = acc[core, which] + acc_got[which]
        if which == 0:
            both = both * scaling
        for g in range(8):
            g_send[g, which] = both[:, g * 128:(g + 1) * 128].astype(BF)
    gs = []
    for step in range(1, 8):
        there = lax.rem(chip + step, 8)
        gs.append(push(g_send.at[there], g_recv.at[step - 1], gr_send.at[step], gr_recv.at[step], device(there, core)))

    gk_ref[:, mine] = g_send[chip, 0].astype(F32).T
    gv_ref[:, mine] = g_send[chip, 1].astype(F32).T
    for step in range(1, 8):
        gs[step - 1].wait_recv()
        columns = pl.ds(pl.multiple_of(lax.rem(chip - step + 8, 8) * 128, 128), 128)
        gk_ref[:, columns] = g_recv[step - 1, 0].astype(F32).T
        gv_ref[:, columns] = g_recv[step - 1, 1].astype(F32).T
    for valid, copy in sent:
        guarded(valid, copy.wait_send)


def place_kernel(*refs):
    sources, targets, sems = refs[:5], refs[5:10], refs[10]
    copies = [
        pltpu.make_async_copy(source, target, sems.at[index])
        for index, (source, target) in enumerate(zip(sources, targets))
    ]
    for copy in copies:
        copy.start()
    for copy in copies:
        copy.wait()


def on_chip_grid(
    layer_input, norm_gain, w_query, w_key, w_value, w_out, cart_key, cart_value, grad_out
):
    half = HD // 2
    frequency = jnp.exp(-jnp.log(500000.0) * jnp.arange(half, dtype=F32) * (2.0 / HD))
    positions = C + jnp.arange(ROWS) % SEQ
    angles = positions.astype(F32)[:, None] * frequency[None, :]
    cosines = jnp.concatenate([jnp.cos(angles), jnp.cos(angles)], 1)
    sines = jnp.concatenate([-jnp.sin(angles), jnp.sin(angles)], 1)
    vmem = pl.BlockSpec(memory_space=pltpu.VMEM)
    hbm = pl.BlockSpec(memory_space=pl.ANY)
    V = pltpu.VMEM
    dma = pltpu.SemaphoreType.DMA
    shapes = (
        jax.ShapeDtypeStruct((256, 512), BF),
        jax.ShapeDtypeStruct((128, 1024), F32),
        jax.ShapeDtypeStruct((128, 1024), F32),
        jax.ShapeDtypeStruct((64, 256), BF),
        jax.ShapeDtypeStruct((64, 256), BF),
    )
    results = pl.pallas_call(
        layer_kernel,
        out_shape=shapes,
        in_specs=[vmem, vmem, vmem, vmem, hbm, hbm, hbm, hbm, vmem, vmem, vmem],
        out_specs=(vmem,) * 5,
        scratch_shapes=[
            V((2, 8, 256, 512), BF), V((2, 8, 256, 512), BF),
            V((8192, 512), BF), V((512, 1024), BF), V((512, 1024), BF), V((512, 8192), BF),
            V((2, 8, 128, 128), BF), V((2, 8, 128, 128), BF), V((16, 8, 256), F32),
            V((8, 2, 128, 128), F32), V((8, 2, 128, 128), F32), V((2, 4, 2, 128, 128), F32),
            V((4, 2, 128, 128), F32), V((4, 2, 128, 128), F32), V((3, 2, 128, 128), F32),
            V((2, 2, 128, 128), BF),
            V((4, 256, 128), BF), V((4, 256, 2048), F32), V((4, 256, 128), BF), V((4, 256, 128), BF),
            V((2, 2, 128, 1024), F32), V((2, 128, 1024), F32),
            V((8, 2, 128, 128), BF), V((7, 2, 128, 128), BF),
            V((8, 256, 512), F32), V((8, 256, 512), F32),
            V((4, 256, 512), BF), V((4, 256, 512), BF), V((3, 256, 512), BF), V((3, 256, 512), BF),
            dma((4,)), dma((15,)), dma((15,)), dma((2, 8)), dma((2, 8)),
            dma((2, 2, 3)), dma((2, 2, 3)), dma((2, 7)), dma((2, 7)), dma((2, 2, 7)), dma((2, 2, 7)),
            dma((9,)), dma((9,)), dma((3, 8)), dma((3, 8)), dma((8,)), dma((8,)),
        ],
        compiler_params=pltpu.CompilerParams(
            collective_id=0, has_side_effects=True, vmem_limit_bytes=63 * 2**20
        ),
        name="attention_layer",
    )(
        layer_input, norm_gain.reshape(1, -1), cosines, sines, w_query, w_key, w_value, w_out,
        cart_key, cart_value, grad_out,
    )
    attn_out, grad_key, grad_value, keys_t, values_t = pl.pallas_call(
        place_kernel,
        out_shape=shapes,
        in_specs=[hbm] * 5,
        out_specs=(hbm,) * 5,
        scratch_shapes=[dma((5,))],
        name="place_results",
    )(*results)
    return attn_out, grad_key, grad_value, keys_t.T, values_t.T


def solution(mesh):
    body = on_chip_grid if mesh.shape["fsdp"] == 16 else on_device
    return jax.shard_map(
        body,
        mesh=mesh,
        in_specs=(
            P("groups", "fsdp"),
            P("fsdp"),
            P(None, "fsdp"),
            P("fsdp", None),
            P("fsdp", None),
            P("fsdp", None),
            P(("groups", "fsdp"), None),
            P(("groups", "fsdp"), None),
            P("groups", "fsdp"),
        ),
        out_specs=(
            P("groups", "fsdp"),
            P(("groups", "fsdp"), None),
            P(("groups", "fsdp"), None),
            P("groups", "fsdp"),
            P("groups", "fsdp"),
        ),
        check_vma=False,
    )
```

```python
import jax
import jax.numpy as jnp
from jax import lax
from jax.experimental import pallas as pl
from jax.experimental.pallas import tpu as pltpu
from jax.sharding import PartitionSpec as P

H = 64
KV = 8
HD = 128
C = 2048
SEQ = 64


def rotate(vectors, positions):
    half_dim = vectors.shape[-1] // 2
    frequency = jnp.exp(
        -jnp.log(500000.0) * jnp.arange(half_dim, dtype=jnp.float32) * (2.0 / vectors.shape[-1])
    )
    angles = positions.astype(jnp.float32)[:, None] * frequency[None, :]
    cosines = jnp.cos(angles)[:, None, :]
    sine_table = jnp.sin(angles)[:, None, :]
    first_half = vectors[..., :half_dim]
    second = vectors[..., half_dim:]
    return jnp.concatenate(
        [first_half * cosines - second * sine_table, second * cosines + first_half * sine_table], -1
    )


def head_block(queries, slot_keys, slot_values, token_keys, token_values, grad_heads, seq_len):
    scaling = queries.shape[-1] ** (-0.5)
    token_count = queries.shape[1]
    score_cart = (
        jnp.einsum("gtd,cd->gtc", queries, slot_keys, preferred_element_type=jnp.float32) * scaling
    )
    score_tok = (
        jnp.einsum("gtd,sd->gts", queries, token_keys, preferred_element_type=jnp.float32) * scaling
    )
    index_rows = jnp.arange(token_count)
    causal = (index_rows[:, None] // seq_len == index_rows[None, :] // seq_len) & (
        index_rows[None, :] <= index_rows[:, None]
    )
    score_tok = jnp.where(causal[None], score_tok, -jnp.inf)
    row_max = jnp.maximum(
        jnp.max(score_cart, -1, keepdims=True), jnp.max(score_tok, -1, keepdims=True)
    )
    exp_cart = jnp.exp(score_cart - row_max)
    exp_tok = jnp.exp(score_tok - row_max)
    totals = jnp.sum(exp_cart, -1, keepdims=True) + jnp.sum(exp_tok, -1, keepdims=True)
    prob_cart = exp_cart / totals
    rounded_cart = prob_cart.astype(jnp.bfloat16)
    rounded_tok = (exp_tok / totals).astype(jnp.bfloat16)
    mixture = jnp.einsum(
        "gtc,cd->gtd", rounded_cart, slot_values, preferred_element_type=jnp.float32
    )
    mixture = mixture + jnp.einsum(
        "gts,sd->gtd", rounded_tok, token_values, preferred_element_type=jnp.float32
    )
    outputs = mixture.astype(jnp.bfloat16)
    grad_prob_cart = jnp.einsum(
        "gtd,cd->gtc", grad_heads, slot_values, preferred_element_type=jnp.float32
    )
    deltas = jnp.sum(
        grad_heads.astype(jnp.float32) * outputs.astype(jnp.float32), -1, keepdims=True
    )
    grad_score = (prob_cart * (grad_prob_cart - deltas)).astype(jnp.bfloat16)
    grad_keys = (
        jnp.einsum("gtc,gtd->cd", grad_score, queries, preferred_element_type=jnp.float32) * scaling
    )
    grad_values = jnp.einsum(
        "gtc,gtd->cd", rounded_cart, grad_heads, preferred_element_type=jnp.float32
    )
    return (outputs, grad_keys, grad_values)


def on_device(
    layer_input, norm_gain, w_query, w_key, w_value, w_out, cart_key, cart_value, grad_out
):
    devices = lax.axis_size("fsdp")
    my_index = lax.axis_index("fsdp")
    token_count = layer_input.shape[0]
    feature_count = layer_input.shape[1]
    local_heads = w_query.shape[1] // HD
    slot_count = cart_key.shape[0]
    kv_width = w_key.shape[1]
    gathered, gathered_gain = (
        lax.all_gather(layer_input, "fsdp", axis=1, tiled=True),
        lax.all_gather(norm_gain, "fsdp", axis=0, tiled=True),
    )
    gathered_f32 = gathered.astype(jnp.float32)
    inverse_rms = lax.rsqrt(jnp.mean(gathered_f32 * gathered_f32, -1, keepdims=True) + 1e-05)
    normed = (gathered_f32 * inverse_rms * gathered_gain.astype(jnp.float32)[None, :]).astype(
        jnp.bfloat16
    )
    own_part = lax.dynamic_slice_in_dim(normed, my_index * feature_count, feature_count, 1)
    partial_kv = jnp.concatenate(
        [
            jnp.dot(own_part, w_key, preferred_element_type=jnp.float32),
            jnp.dot(own_part, w_value, preferred_element_type=jnp.float32),
        ],
        1,
    )
    token_kv = lax.psum(partial_kv, "fsdp")
    positions = C + jnp.arange(token_count) % SEQ
    all_token_keys = (
        rotate(token_kv[:, :kv_width].reshape(token_count, kv_width // HD, HD), positions)
        .reshape(token_count, kv_width)
        .astype(jnp.bfloat16)
    )
    all_token_values = token_kv[:, kv_width:].astype(jnp.bfloat16)
    column_count = kv_width // devices
    new_keys = lax.dynamic_slice_in_dim(all_token_keys, my_index * column_count, column_count, 1)
    new_values = lax.dynamic_slice_in_dim(
        all_token_values, my_index * column_count, column_count, 1
    )
    kv_group = my_index * local_heads // (H // KV)
    token_keys = lax.dynamic_slice_in_dim(all_token_keys, kv_group * HD, HD, 1)
    token_values = lax.dynamic_slice_in_dim(all_token_values, kv_group * HD, HD, 1)
    queries = jnp.dot(normed, w_query, preferred_element_type=jnp.float32).reshape(
        token_count, local_heads, HD
    )
    queries = rotate(queries, positions).astype(jnp.bfloat16).transpose(1, 0, 2)
    spread_keys = jnp.repeat(cart_key.reshape(slot_count, KV, HD), devices // KV, axis=1)
    spread_values = jnp.repeat(cart_value.reshape(slot_count, KV, HD), devices // KV, axis=1)
    own_slots = lax.all_to_all(
        jnp.concatenate([spread_keys, spread_values], 2),
        "fsdp",
        split_axis=1,
        concat_axis=0,
        tiled=True,
    )
    slot_keys = own_slots[:, 0, :HD]
    slot_values = own_slots[:, 0, HD:]
    cotangent = lax.all_gather(grad_out, "fsdp", axis=1, tiled=True)
    grad_heads = lax.dot_general(
        cotangent, w_out, (((1,), (1,)), ((), ())), preferred_element_type=jnp.float32
    )
    grad_heads = (
        grad_heads.astype(jnp.bfloat16).reshape(token_count, local_heads, HD).transpose(1, 0, 2)
    )
    outputs, grad_keys, grad_values = head_block(
        queries, slot_keys, slot_values, token_keys, token_values, grad_heads, SEQ
    )
    head_outputs = outputs.transpose(1, 0, 2).reshape(token_count, local_heads * HD)
    partial_out = jnp.dot(head_outputs, w_out, preferred_element_type=jnp.float32)
    attn_out = lax.psum_scatter(partial_out, "fsdp", scatter_dimension=1, tiled=True).astype(
        jnp.bfloat16
    )
    total_slots = grad_keys.shape[0]
    stacked = jnp.concatenate([grad_keys, grad_values], 1).reshape(
        devices, total_slots // devices, 2 * HD
    )
    received = lax.all_to_all(stacked, "fsdp", split_axis=0, concat_axis=0, tiled=True)
    summed = jnp.sum(
        received.reshape(KV, devices // KV, total_slots // devices, 2 * HD), axis=1
    ).transpose(1, 0, 2)
    grad_key = summed[:, :, :HD].reshape(total_slots // devices, KV * HD)
    grad_value = summed[:, :, HD:].reshape(total_slots // devices, KV * HD)
    return (attn_out, grad_key, grad_value, new_keys, new_values)


BF = jnp.bfloat16
F32 = jnp.float32
ROWS = 128


def dot(a, b):
    return jnp.dot(a, b, preferred_element_type=F32)


def dot_t(a, b):
    return lax.dot_general(a, b, (((1,), (1,)), ((), ())), preferred_element_type=F32)


def layer_kernel(
    x_ref, gain_ref, cos_ref, sin_ref, wq_hbm, wk_hbm, wv_hbm, wo_hbm, ck_ref, cv_ref, go_ref,
    out_ref, gk_ref, gv_ref, nk_ref, nv_ref,
    normed, cot, wq, wk, wv, wo, slot_k, slot_v, squares,
    kv_swap, kv_got, kv_send, kv_y, kv_z, kv_recv, tok,
    queries, probs, heads, grads, acc, acc_got, g_send, g_recv,
    o_swap, o_got, y_send, y_recv, z_send, z_recv,
    load_sem, sq_send, sq_recv, cart_send, cart_recv, n_send, n_recv, yg_send, yg_recv, c_send, c_recv,
    kv_ssem, kv_rsem, os_send, os_recv, gr_send, gr_recv,
):
    me = lax.axis_index("fsdp")
    core = lax.rem(me, 2)
    chip = me // 2
    ydim = lax.rem(chip, 2)
    zdim = chip // 2
    other = 1 - core

    def device(chip_index, core_index):
        return {"fsdp": chip_index * 2 + core_index}

    def zchip(steps, yy):
        return lax.rem(zdim + steps + 4, 4) * 2 + yy

    def remote(source, target, send, recv, where):
        return pltpu.make_async_remote_copy(
            src_ref=source, dst_ref=target, send_sem=send, recv_sem=recv,
            device_id=where, device_id_type=pl.DeviceIdType.MESH,
        )

    sent = []

    def guarded(valid, action):
        if valid is None:
            action()
        else:
            pl.when(valid)(action)

    def push(source, target, send, recv, where, valid=None):
        copy = remote(source, target, send, recv, where)
        guarded(valid, copy.start)
        sent.append((valid, copy))
        return copy

    loads = [
        pltpu.make_async_copy(source, target, load_sem.at[index])
        for index, (source, target) in enumerate(
            [(wk_hbm, wk), (wv_hbm, wv), (wq_hbm, wq), (wo_hbm, wo)]
        )
    ]
    for load in loads:
        load.start()

    barrier = pltpu.get_barrier_semaphore()
    for step in range(1, 16):
        pl.semaphore_signal(
            barrier, inc=1, device_id={"fsdp": lax.rem(me + step, 16)},
            device_id_type=pl.DeviceIdType.MESH,
        )

    x = x_ref[...].astype(F32)
    own = jnp.sum(x * x, axis=1, keepdims=True)
    squares[0] = jnp.broadcast_to(own, (256, 128)).T[:8]
    pl.semaphore_wait(barrier, 15)

    sq = [
        push(squares.at[0], squares.at[step], sq_send.at[step - 1], sq_recv.at[step - 1],
             {"fsdp": lax.rem(me + step, 16)})
        for step in range(1, 16)
    ]

    cart = []
    for step in range(1, 8):
        there = lax.rem(chip + step, 8)
        columns = pl.ds(pl.multiple_of(there * 128, 128), 128)
        cart.append(push(ck_ref.at[:, columns], slot_k.at[core, chip], cart_send.at[0, step],
                         cart_recv.at[0, step], device(there, core)))
        cart.append(push(cv_ref.at[:, columns], slot_v.at[core, chip], cart_send.at[1, step],
                         cart_recv.at[1, step], device(there, core)))
    mine = pl.ds(pl.multiple_of(chip * 128, 128), 128)
    slot_k[core, chip] = ck_ref[:, mine]
    slot_v[core, chip] = cv_ref[:, mine]

    for copy in sq:
        copy.wait_recv()
    total = squares[0]
    for step in range(1, 16):
        total = total + squares[step]
    total = jnp.broadcast_to(total[:1], (128, 256)).T[:, :1]
    inverse = lax.rsqrt(total * (1.0 / 8192.0) + 1e-05)
    normed[core, chip] = (
        x_ref[...].astype(F32) * inverse * gain_ref[...].astype(F32)
    ).astype(BF)
    cot[core, chip] = go_ref[...]

    above = device(zchip(1, ydim), core)
    below = device(zchip(-1, ydim), core)
    across = device(zdim * 2 + 1 - ydim, core)
    twin = device(chip, other)

    def arrivals(step):
        return (
            (0, -1 - step, zdim >= 1 + step, (zdim >= 1 + step) & (zdim < 3), above),
            (1, 1 + step, zdim < 3 - step, (zdim < 3 - step) & (zdim > 0), below),
        )

    def gather_start(buffer, k):
        slot = buffer.at[core, chip]
        push(slot, slot, n_send.at[k, 0, 0], n_recv.at[k, 0, 0], above, zdim < 3)
        push(slot, slot, n_send.at[k, 1, 0], n_recv.at[k, 1, 0], below, zdim > 0)
        push(slot, slot, yg_send.at[k, 6], yg_recv.at[k, 6], across)
        push(slot, slot, c_send.at[k, 0, 6], c_recv.at[k, 0, 6], twin)

    def gather_step(buffer, k, step):
        for way, offset, here, further, onward in arrivals(step):
            slot = buffer.at[core, zchip(offset, ydim)]
            number = way * 3 + step
            arrived = remote(slot, slot, n_send.at[k, way, step], n_recv.at[k, way, step], onward)
            guarded(here, arrived.wait_recv)
            if step < 2:
                push(slot, slot, n_send.at[k, way, step + 1], n_recv.at[k, way, step + 1], onward, further)
            push(slot, slot, yg_send.at[k, number], yg_recv.at[k, number], across, here)
            push(slot, slot, c_send.at[k, 0, number], c_recv.at[k, 0, number], twin, here)

    def gather_across(buffer, k, steps):
        for step in steps:
            pairs = [(6, 0, None)] if step < 0 else [
                (way * 3 + step, offset, here) for way, offset, here, _, _ in arrivals(step)
            ]
            for number, offset, here in pairs:
                slot = buffer.at[core, zchip(offset, 1 - ydim)]
                arrived = remote(slot, slot, yg_send.at[k, number], yg_recv.at[k, number], across)
                guarded(here, arrived.wait_recv)
                push(slot, slot, c_send.at[k, 1, number], c_recv.at[k, 1, number], twin, here)

    def gather_finish(buffer, k):
        for step in (-1, 0, 1, 2):
            pairs = [(6, 0, None)] if step < 0 else [
                (way * 3 + step, offset, here) for way, offset, here, _, _ in arrivals(step)
            ]
            for number, offset, here in pairs:
                for part in range(2):
                    slot = buffer.at[other, zchip(offset, ydim if part == 0 else 1 - ydim)]
                    arrived = remote(slot, slot, c_send.at[k, part, number], c_recv.at[k, part, number], twin)
                    guarded(here, arrived.wait_recv)

    gather_start(normed, 0)

    loads[0].wait()
    loads[1].wait()

    def partial_kv(g, tokens_of):
        rows = pl.ds(pl.multiple_of(tokens_of * ROWS, ROWS), ROWS)
        columns = pl.ds(pl.multiple_of(g * 128, 128), 128)
        left = normed[core, chip, rows, :]
        return dot(left, wk[:, columns]), dot(left, wv[:, columns])

    @pl.loop(0, 8)
    def _(g):
        a, b = partial_kv(g, other)
        kv_swap[g, 0] = a
        kv_swap[g, 1] = b

    swap = push(kv_swap, kv_got, kv_ssem.at[0], kv_rsem.at[0], device(chip, other))
    gather_step(normed, 0, 0)
    swap.wait_recv()

    @pl.loop(0, 8)
    def _(g):
        a, b = partial_kv(g, core)
        yy, zz = lax.rem(g, 2), g // 2
        kv_send[yy, zz, 0] = a + kv_got[g, 0]
        kv_send[yy, zz, 1] = b + kv_got[g, 1]

    kv_across = push(kv_send.at[1 - ydim], kv_y, kv_ssem.at[1], kv_rsem.at[1], across)
    gather_step(normed, 0, 1)
    gather_across(normed, 0, (-1,))
    gather_step(normed, 0, 2)
    gather_start(cot, 1)
    gather_across(normed, 0, (0,))
    kv_across.wait_recv()
    kv = []
    for d in (1, 2, 3, 0):
        zz = lax.rem(zdim + d, 4)
        kv_z[d] = kv_send[ydim, zz] + kv_y[zz]
        if d:
            kv.append(push(kv_z.at[d], kv_recv.at[d - 1], kv_ssem.at[1 + d], kv_rsem.at[1 + d], device(zchip(d, ydim), core)))
    gather_across(normed, 0, (1,))
    gather_step(cot, 1, 0)
    gather_across(normed, 0, (2,))
    gather_finish(normed, 0)

    loads[2].wait()

    def project(source, weight):
        def body(index, total):
            cc, g = index // 8, lax.rem(index, 8)
            rows = pl.ds(pl.multiple_of((g * 2 + cc) * 512, 512), 512)
            return total + dot(source[cc, g], weight[rows, :])
        return lax.fori_loop(0, 16, body, jnp.zeros((256, 512), F32))

    cosines = cos_ref[...]
    sines = sin_ref[...]

    def rotated(v, c, s):
        return v * c + pltpu.roll(v, 64, 1) * s

    cos2 = jnp.concatenate([cosines, cosines], 0)
    sin2 = jnp.concatenate([sines, sines], 0)
    q_all = project(normed, wq)
    for h in range(4):
        queries[h] = rotated(q_all[:, h * 128:(h + 1) * 128], cos2, sin2).astype(BF)

    gather_step(cot, 1, 1)
    for copy in cart:
        copy.wait_recv()
    swap_k = push(slot_k.at[core], slot_k.at[core], cart_send.at[0, 0], cart_recv.at[0, 0], device(chip, other))
    swap_v = push(slot_v.at[core], slot_v.at[core], cart_send.at[1, 0], cart_recv.at[1, 0], device(chip, other))
    for copy in kv:
        copy.wait_recv()
    key_sum = kv_z[0, 0]
    value_sum = kv_z[0, 1]
    for step in range(3):
        key_sum = key_sum + kv_recv[step, 0]
        value_sum = value_sum + kv_recv[step, 1]
    tok[core, 0] = rotated(key_sum, cosines, sines).astype(BF)
    tok[core, 1] = value_sum.astype(BF)
    swap_t = push(tok.at[core], tok.at[core], kv_ssem.at[8], kv_rsem.at[8], device(chip, other))
    gather_step(cot, 1, 2)
    swap_t.wait_recv()
    for half in range(2):
        tokens = slice(half * ROWS, (half + 1) * ROWS)
        for which, target in ((0, nk_ref), (1, nv_ref)):
            block = tok[half, which].astype(F32).T
            target[:, tokens] = jnp.where(core == 0, block[:64], block[64:]).astype(BF)
    swap_k.wait_recv()
    swap_v.wait_recv()

    scaling = HD ** (-0.5)
    token_row = lax.broadcasted_iota(jnp.int32, (ROWS, ROWS), 0)
    token_col = lax.broadcasted_iota(jnp.int32, (ROWS, ROWS), 1)
    causal = (token_row // SEQ == token_col // SEQ) & (token_col <= token_row)

    def attend(index):
        h, half = index // 2, lax.rem(index, 2)
        rows = pl.ds(pl.multiple_of(half * ROWS, ROWS), ROWS)
        q = queries[h, rows, :]
        keys = slot_k[...].reshape(C, HD)
        score = dot_t(q, keys) * scaling
        score_tok = jnp.where(causal, dot_t(q, tok[half, 0]) * scaling, -jnp.inf)
        top = jnp.maximum(
            jnp.max(score, -1, keepdims=True), jnp.max(score_tok, -1, keepdims=True)
        )
        e = jnp.exp(score - top)
        e_tok = jnp.exp(score_tok - top)
        inv = 1.0 / (jnp.sum(e, -1, keepdims=True) + jnp.sum(e_tok, -1, keepdims=True))
        p = e * inv
        probs[h, rows, :] = p
        mixture = dot(p.astype(BF), slot_v[...].reshape(C, HD))
        mixture = mixture + dot((e_tok * inv).astype(BF), tok[half, 1])
        heads[h, rows, :] = mixture.astype(BF)

    pl.loop(0, 4)(attend)
    gather_across(cot, 1, (-1, 0))
    pl.loop(4, 8)(attend)

    loads[3].wait()
    all_heads = jnp.concatenate([heads[h] for h in range(4)], 1)

    def partial_out(g, cc):
        columns = pl.ds(pl.multiple_of((g * 2 + cc) * 512, 512), 512)
        return dot(all_heads, wo[:, columns])

    swaps = []
    for index, (d, yy) in enumerate([(d, k) for k in (1, 0) for d in (1, 2, 3, 0)]):
        g = zchip(d, 1 - ydim if yy else ydim)
        o_swap[index] = partial_out(g, other)
        swaps.append(push(o_swap.at[index], o_got.at[index], os_send.at[0, index], os_recv.at[0, index], device(chip, other)))
    ys = []
    for index, d in enumerate((1, 2, 3, 0)):
        part = partial_out(zchip(d, 1 - ydim), core)
        swaps[index].wait_recv()
        y_send[index] = (part + o_got[index]).astype(BF)
        ys.append(push(y_send.at[index], y_recv.at[index], os_send.at[1, index], os_recv.at[1, index], device(zdim * 2 + 1 - ydim, core)))

    gather_across(cot, 1, (1, 2))
    gather_finish(cot, 1)

    def grad_body(index, total):
        cc, g = index // 8, lax.rem(index, 8)
        columns = pl.ds(pl.multiple_of((g * 2 + cc) * 512, 512), 512)
        return total + dot_t(cot[cc, g], wo[:, columns])

    g_all = lax.fori_loop(0, 16, grad_body, jnp.zeros((256, 512), F32)).astype(BF)
    for h in range(4):
        grads[h] = g_all[:, h * 128:(h + 1) * 128]

    acc[...] = jnp.zeros_like(acc)

    def differentiate(index):
        h, half = index // 2, lax.rem(index, 2)
        rows = pl.ds(pl.multiple_of(half * ROWS, ROWS), ROWS)
        q_t = queries[h, rows, :].T
        gh = grads[h, rows, :]
        gh_t = gh.T
        delta = jnp.sum(gh.astype(F32) * heads[h, rows, :].astype(F32), -1, keepdims=True)
        for cc in range(2):
            values = slot_v[cc].reshape(C // 2, HD)
            p = probs[h, rows, cc * (C // 2):(cc + 1) * (C // 2)]
            score = (p * (dot_t(gh, values) - delta)).astype(BF)
            acc[cc, 0] += dot(q_t, score)
            acc[cc, 1] += dot(gh_t, p.astype(BF))

    zs = []
    for index, d in enumerate((1, 2, 3)):
        pl.loop(2 * index, 2 * index + 2)(differentiate)
        part = partial_out(zchip(d, ydim), core)
        swaps[4 + index].wait_recv()
        ys[index].wait_recv()
        z_send[index] = (part + o_got[4 + index] + y_recv[index].astype(F32)).astype(BF)
        zs.append(push(z_send.at[index], z_recv.at[index], os_send.at[2, index], os_recv.at[2, index], device(zchip(d, ydim), core)))
    pl.loop(6, 8)(differentiate)

    swap_a = push(acc.at[other], acc_got, gr_send.at[0], gr_recv.at[0], device(chip, other))

    swap_a.wait_recv()
    for which in range(2):
        both = acc[core, which] + acc_got[which]
        if which == 0:
            both = both * scaling
        for g in range(8):
            g_send[g, which] = both[:, g * 128:(g + 1) * 128].astype(BF)
    gs = []
    for step in range(1, 8):
        there = lax.rem(chip + step, 8)
        gs.append(push(g_send.at[there], g_recv.at[step - 1], gr_send.at[step], gr_recv.at[step], device(there, core)))

    part = partial_out(chip, core)
    swaps[7].wait_recv()
    ys[3].wait_recv()
    part = part + o_got[7] + y_recv[3].astype(F32)
    for index in range(3):
        zs[index].wait_recv()
        part = part + z_recv[index].astype(F32)
    out_ref[...] = part.astype(BF)

    gk_ref[:, mine] = g_send[chip, 0].astype(F32).T
    gv_ref[:, mine] = g_send[chip, 1].astype(F32).T
    for step in range(1, 8):
        gs[step - 1].wait_recv()
        columns = pl.ds(pl.multiple_of(lax.rem(chip - step + 8, 8) * 128, 128), 128)
        gk_ref[:, columns] = g_recv[step - 1, 0].astype(F32).T
        gv_ref[:, columns] = g_recv[step - 1, 1].astype(F32).T
    for valid, copy in sent:
        guarded(valid, copy.wait_send)


def place_kernel(*refs):
    for source, target in zip(refs[:5], refs[5:]):
        target[...] = source[...]


def on_chip_grid(
    layer_input, norm_gain, w_query, w_key, w_value, w_out, cart_key, cart_value, grad_out
):
    half = HD // 2
    frequency = jnp.exp(-jnp.log(500000.0) * jnp.arange(half, dtype=F32) * (2.0 / HD))
    positions = C + jnp.arange(ROWS) % SEQ
    angles = positions.astype(F32)[:, None] * frequency[None, :]
    cosines = jnp.concatenate([jnp.cos(angles), jnp.cos(angles)], 1)
    sines = jnp.concatenate([-jnp.sin(angles), jnp.sin(angles)], 1)
    vmem = pl.BlockSpec(memory_space=pltpu.VMEM)
    hbm = pl.BlockSpec(memory_space=pl.ANY)
    V = pltpu.VMEM
    dma = pltpu.SemaphoreType.DMA
    shapes = (
        jax.ShapeDtypeStruct((256, 512), BF),
        jax.ShapeDtypeStruct((128, 1024), F32),
        jax.ShapeDtypeStruct((128, 1024), F32),
        jax.ShapeDtypeStruct((64, 256), BF),
        jax.ShapeDtypeStruct((64, 256), BF),
    )
    results = pl.pallas_call(
        layer_kernel,
        out_shape=shapes,
        in_specs=[vmem, vmem, vmem, vmem, hbm, hbm, hbm, hbm, vmem, vmem, vmem],
        out_specs=(vmem,) * 5,
        scratch_shapes=[
            V((2, 8, 256, 512), BF), V((2, 8, 256, 512), BF),
            V((8192, 512), BF), V((512, 1024), BF), V((512, 1024), BF), V((512, 8192), BF),
            V((2, 8, 128, 128), BF), V((2, 8, 128, 128), BF), V((16, 8, 256), F32),
            V((8, 2, 128, 128), F32), V((8, 2, 128, 128), F32), V((2, 4, 2, 128, 128), F32),
            V((4, 2, 128, 128), F32), V((4, 2, 128, 128), F32), V((3, 2, 128, 128), F32),
            V((2, 2, 128, 128), BF),
            V((4, 256, 128), BF), V((4, 256, 2048), F32), V((4, 256, 128), BF), V((4, 256, 128), BF),
            V((2, 2, 128, 1024), F32), V((2, 128, 1024), F32),
            V((8, 2, 128, 128), BF), V((7, 2, 128, 128), BF),
            V((8, 256, 512), F32), V((8, 256, 512), F32),
            V((4, 256, 512), BF), V((4, 256, 512), BF), V((3, 256, 512), BF), V((3, 256, 512), BF),
            dma((4,)), dma((15,)), dma((15,)), dma((2, 8)), dma((2, 8)),
            dma((2, 2, 3)), dma((2, 2, 3)), dma((2, 7)), dma((2, 7)), dma((2, 2, 7)), dma((2, 2, 7)),
            dma((9,)), dma((9,)), dma((3, 8)), dma((3, 8)), dma((8,)), dma((8,)),
        ],
        compiler_params=pltpu.CompilerParams(
            collective_id=0, has_side_effects=True, vmem_limit_bytes=63 * 2**20
        ),
        name="attention_layer",
    )(
        layer_input, norm_gain.reshape(1, -1), cosines, sines, w_query, w_key, w_value, w_out,
        cart_key, cart_value, grad_out,
    )
    attn_out, grad_key, grad_value, keys_t, values_t = pl.pallas_call(
        place_kernel,
        out_shape=shapes,
        in_specs=[vmem] * 5,
        out_specs=(vmem,) * 5,
        name="place_results",
    )(*results)
    return attn_out, grad_key, grad_value, keys_t.T, values_t.T


def solution(mesh):
    body = on_chip_grid if mesh.shape["fsdp"] == 16 else on_device
    return jax.shard_map(
        body,
        mesh=mesh,
        in_specs=(
            P("groups", "fsdp"),
            P("fsdp"),
            P(None, "fsdp"),
            P("fsdp", None),
            P("fsdp", None),
            P("fsdp", None),
            P(("groups", "fsdp"), None),
            P(("groups", "fsdp"), None),
            P("groups", "fsdp"),
        ),
        out_specs=(
            P("groups", "fsdp"),
            P(("groups", "fsdp"), None),
            P(("groups", "fsdp"), None),
            P("groups", "fsdp"),
            P("groups", "fsdp"),
        ),
        check_vma=False,
    )
```
